32 devices in a mesh: row: 4 (over y, x), col: 8 (over z, core).
Axes of the slice: x: 2, y: 2, z: 4, core: 2. Of those that a mesh axis runs over, the one named last changes fastest.
Arguments:
- teacher: bfloat16 [16384, 256], replicated, may hold values from -4 to 4
- panel_ids: int32 [2048], P('col'), may hold values from 0 to 16383
- rest_ids: int32 [4, 8, 128], P('row', 'col'), may hold values from 0 to 16383
- inverse: bfloat16 [2048, 2048], replicated, may hold values from -1 to 1, as said below
Outputs:
- trailing: float32 [8, 4, 128, 4, 8, 128], P(None, 'row', None, None, 'col')
- panel_rows: bfloat16 [4, 8, 128, 2048], P('row', 'col')
The draws below stay inside these ranges and needn't reach their ends.
Inputs may be any that keep to these rules, and one draw needn't show every extreme that they name: `inverse`: zero above the diagonal.
All inputs are finite; a program needn't handle non-finite values.
Results may differ from the reference program's by a relative error of at most 0.0049.
Values may be sent and summed in bfloat16 or wider, within the bound.
A program may use at most 128 MiB of HBM per device.

```python
import math
import jax
import jax.numpy as jnp
from jax import lax

E = 256
P_SIZE = 2048
VOCAB = 16384
STRETCH = 128
N_ROW = 4
N_COL = 8


def draw_teacher(key, part):
    first_key, second_key = jax.random.split(key, 2)
    groups = 16
    repeats = E // groups
    coords = jnp.clip(jax.random.normal(first_key, (VOCAB, groups), jnp.float32) * math.sqrt(0.5), -3.0, 3.0)
    noise = jnp.clip(0.2 * jax.random.normal(second_key, (VOCAB, E), jnp.float32), -0.8, 0.8)
    tiled = jnp.broadcast_to(coords[:, None, :], (VOCAB, repeats, groups)).reshape(VOCAB, E)
    return jnp.clip(tiled + noise, -4.0, 4.0).astype(jnp.bfloat16)


def draw_inverse(key, part):
    first_key, second_key = jax.random.split(key, 2)
    diagonal = jnp.exp(jax.random.uniform(first_key, (P_SIZE,), jnp.float32, math.log(0.5), math.log(2.0)))
    offdiag = jnp.clip(jax.random.normal(second_key, (P_SIZE, P_SIZE), jnp.float32), -4.0, 4.0)
    places = jnp.arange(P_SIZE)
    lower = places[:, None] > places[None, :]
    matrix = jnp.where(lower, offdiag / math.sqrt(P_SIZE), 0.0) + jnp.diag(diagonal)
    return (matrix * (5.0 / math.sqrt(P_SIZE))).astype(jnp.bfloat16)


def plant(values, rng, low, largest):
    place = [jax.random.randint(jax.random.fold_in(rng, axis), (), 0, length) for axis, length in enumerate(values.shape)]
    main_axis = values.shape.index(max(values.shape))
    neighbour = place[:main_axis] + [(place[main_axis] + 1) % values.shape[main_axis]] + place[main_axis + 1:]
    return values.at[tuple(place)].set(low).at[tuple(neighbour)].set(largest)


def setup_inputs(seed: int = 0) -> dict:
    splits = jax.random.split(jax.random.key(seed), 5)
    teacher = draw_teacher(jax.random.fold_in(splits[4], 71), 0)
    panel_ids = plant(jax.random.randint(splits[1], (P_SIZE,), 0, VOCAB), jax.random.fold_in(splits[1], 1), 0, VOCAB - 1).astype(jnp.int32)
    rest_ids = plant(jax.random.randint(splits[2], (N_ROW, N_COL, STRETCH), 0, VOCAB), jax.random.fold_in(splits[2], 1), 0, VOCAB - 1).astype(jnp.int32)
    inverse = draw_inverse(jax.random.fold_in(splits[4], 71), 0)
    return {"teacher": teacher, "panel_ids": panel_ids, "rest_ids": rest_ids, "inverse": inverse}


def gaussian(left_rows, right_rows, inv_scale):
    sq_left = jnp.sum(jnp.square(left_rows.astype(jnp.float32)), axis=-1)
    sq_right = jnp.sum(jnp.square(right_rows.astype(jnp.float32)), axis=-1)
    inner = lax.dot_general(left_rows, right_rows, (((1,), (1,)), ((), ())), preferred_element_type=jnp.float32)
    return jnp.exp(-inv_scale * (sq_left[:, None] + sq_right[None, :] - 2.0 * inner))


def reference(teacher, panel_ids, rest_ids, inverse):
    inv_scale = 2.0 / E
    panel_emb = teacher[panel_ids]
    rest_emb = teacher[rest_ids.reshape(-1)]
    kernel = gaussian(rest_emb, panel_emb, inv_scale).astype(jnp.bfloat16)
    factors = lax.dot_general(kernel, inverse, (((1,), (1,)), ((), ())), preferred_element_type=jnp.float32).astype(jnp.bfloat16)
    total = rest_emb.shape[0]
    span = total // N_COL

    def one_block(block_at):
        first_row = block_at * span
        left_emb = lax.dynamic_slice_in_dim(rest_emb, first_row, span, 0)
        left_factor = lax.dynamic_slice_in_dim(factors, first_row, span, 0)
        update = lax.dot_general(left_factor, factors, (((1,), (1,)), ((), ())), preferred_element_type=jnp.float32)
        result = gaussian(left_emb, rest_emb, inv_scale) - update
        row_index = first_row + jnp.arange(span, dtype=jnp.int32)
        col_index = jnp.arange(total, dtype=jnp.int32)
        return jnp.where(row_index[:, None] >= col_index[None, :], result, jnp.zeros_like(result))

    full = lax.map(one_block, jnp.arange(N_COL, dtype=jnp.int32))
    trailing = full.reshape(N_COL, N_ROW, STRETCH, N_ROW, N_COL, STRETCH)
    return trailing, factors.reshape(N_ROW, N_COL, STRETCH, P_SIZE)
```

```python
import functools

import jax
import jax.numpy as jnp
from jax import lax
from jax.experimental import pallas as pl
from jax.experimental.pallas import tpu as pltpu
from jax.sharding import PartitionSpec as P

MESH = pl.DeviceIdType.MESH


def exchange_kernel(n_row, n_col, rest_ref, panel_ref, panel_out, row_out, col_out, send_sem, row_sem, col_sem, panel_sem):
    row_at = lax.axis_index("row")
    col_at = lax.axis_index("col")
    me = row_at * n_col + col_at
    barrier = pltpu.get_barrier_semaphore()
    count = n_row * n_col

    def greet(step, carry):
        other = lax.rem(me + step, count)
        pl.semaphore_signal(
            barrier, inc=1, device_id=(other // n_col, lax.rem(other, n_col)), device_id_type=MESH
        )
        return carry

    lax.fori_loop(1, count, greet, 0)
    panel_out[col_at] = panel_ref[0]
    col_out[row_at] = rest_ref[0]
    row_role = lax.rem(me, n_row)
    place = me // n_row

    @pl.when(row_role == row_at)
    def _():
        row_out[place] = rest_ref[0]

    pl.semaphore_wait(barrier, count - 1)

    def panel_copy(slot, target):
        return pltpu.make_async_remote_copy(
            src_ref=panel_ref.at[0], dst_ref=panel_out.at[slot],
            send_sem=send_sem.at[target], recv_sem=panel_sem.at[slot],
            device_id=(row_at, target), device_id_type=MESH,
        )

    def row_copy(slot, target):
        return pltpu.make_async_remote_copy(
            src_ref=rest_ref.at[0], dst_ref=row_out.at[slot],
            send_sem=send_sem.at[n_col + target], recv_sem=row_sem.at[slot],
            device_id=(row_role, target), device_id_type=MESH,
        )

    def col_copy(slot, target):
        return pltpu.make_async_remote_copy(
            src_ref=rest_ref.at[0], dst_ref=col_out.at[slot],
            send_sem=send_sem.at[2 * n_col + target], recv_sem=col_sem.at[slot],
            device_id=(target, col_at), device_id_type=MESH,
        )

    def each(length, skip, act):
        for at in range(length):
            pl.when(jnp.logical_not(skip(at)))(functools.partial(act, at))

    to_self = lambda at: jnp.logical_and(row_role == row_at, at == col_at)
    from_self = lambda at: at * n_row + row_at == me
    each(n_col, lambda at: at == col_at, lambda at: panel_copy(col_at, at).start())
    each(n_col, to_self, lambda at: row_copy(place, at).start())
    each(n_row, lambda at: at == row_at, lambda at: col_copy(row_at, at).start())
    each(n_col, lambda at: at == col_at, lambda at: panel_copy(at, at).wait_recv())
    each(n_col, from_self, lambda at: row_copy(at, at).wait_recv())
    each(n_row, lambda at: at == row_at, lambda at: col_copy(at, at).wait_recv())
    each(n_col, lambda at: at == col_at, lambda at: panel_copy(col_at, at).wait_send())
    each(n_col, to_self, lambda at: row_copy(place, at).wait_send())
    each(n_row, lambda at: at == row_at, lambda at: col_copy(row_at, at).wait_send())


def exchange(rest_ids, panel_ids, n_row, n_col):
    stretch = rest_ids.shape[2]
    width = panel_ids.shape[0]
    vmem = pl.BlockSpec(memory_space=pltpu.VMEM)
    return pl.pallas_call(
        functools.partial(exchange_kernel, n_row, n_col),
        out_shape=(
            jax.ShapeDtypeStruct((n_col, 1, width), jnp.int32),
            jax.ShapeDtypeStruct((n_col, 1, stretch), jnp.int32),
            jax.ShapeDtypeStruct((n_row, 1, stretch), jnp.int32),
        ),
        in_specs=[vmem] * 2,
        out_specs=(vmem,) * 3,
        scratch_shapes=[
            pltpu.SemaphoreType.DMA((2 * n_col + n_row,)),
            pltpu.SemaphoreType.DMA((n_col,)),
            pltpu.SemaphoreType.DMA((n_row,)),
            pltpu.SemaphoreType.DMA((n_col,)),
        ],
        compiler_params=pltpu.CompilerParams(collective_id=0, has_side_effects=True),
        name="exchange",
    )(rest_ids, panel_ids.reshape(1, 1, width))


def nt_dot(left, right):
    return lax.dot_general(left, right, (((1,), (1,)), ((), ())), preferred_element_type=jnp.float32)


def gram_kernel(n_row, n_col, stretch, emb_ref, inv_hbm, trail_ref, own_ref, inv_ref, cross_ref, fac_ref, norm_ref, inv_sem):
    width = inv_hbm.shape[0]
    block = 256
    blocks = width // block
    total = emb_ref.shape[0] - width
    n_rows = n_col * stretch
    unit = 2.0 / emb_ref.shape[1] * 1.4426950408889634
    row_at = lax.axis_index("row")
    col_at = lax.axis_index("col")

    def load(at):
        rows, cols = pl.ds(at * block, block), pl.ds(0, (at + 1) * block)
        return pltpu.make_async_copy(inv_hbm.at[rows, cols], inv_ref.at[rows, cols], inv_sem.at[at])

    for at in range(blocks):
        load(at).start()

    def across(value):
        square = jnp.square(value.astype(jnp.float32))
        high = square.astype(jnp.bfloat16)
        low = (square - high.astype(jnp.float32)).astype(jnp.bfloat16)
        ones = jnp.ones((8, value.shape[1]), jnp.bfloat16)
        return (nt_dot(ones, high) + nt_dot(ones, low)) * unit

    def down(value):
        return jnp.sum(jnp.square(value.astype(jnp.float32)), axis=-1, keepdims=True) * unit

    for at in range(blocks):
        norm_ref[:, at * block : (at + 1) * block] = across(emb_ref[at * block : (at + 1) * block, :])

    def gram(left, left_norm, right, right_norm):
        return jnp.exp2(nt_dot(left, right) * (2.0 * unit) - (left_norm + right_norm))

    tile = 512

    def factor_tile(start, first):
        rows = pl.ds(start, tile)
        left = emb_ref[pl.ds(width + start, tile), :]
        left_norm = down(left)
        for at in range(blocks):
            cols = slice(at * block, (at + 1) * block)
            cross_ref[:, cols] = gram(left, left_norm, emb_ref[cols, :], norm_ref[0:1, cols]).astype(jnp.bfloat16)
            if first:
                load(at).wait()
            fac_ref[rows, cols] = nt_dot(
                cross_ref[:, : (at + 1) * block], inv_ref[cols, : (at + 1) * block]
            ).astype(jnp.bfloat16)

    factor_tile(n_rows, True)
    for start in range(n_rows + tile, total, tile):
        factor_tile(start, False)
    own_ref[...] = fac_ref[pl.ds(pl.multiple_of(n_rows + row_at * stretch, stretch), stretch), :]

    ahead = lax.broadcasted_iota(jnp.int32, (stretch, stretch), 0) - lax.broadcasted_iota(
        jnp.int32, (stretch, stretch), 1
    )
    pair = 2 if n_row % 2 == 0 else 1
    for start in range(0, n_rows, tile):
        factor_tile(start, False)
        left = emb_ref[pl.ds(width + start, tile), :]
        left_norm = down(left)
        last = (start + tile) // stretch - 1
        for low in range(0, n_row, pair):
            if last * n_row + n_row - 1 >= low * n_col:
                first_col = n_rows + low * stretch
                span = pl.ds(first_col, pair * stretch)
                right = emb_ref[pl.ds(width + first_col, pair * stretch), :]
                value = gram(left, left_norm, right, across(right)[0:1]) - nt_dot(
                    fac_ref[pl.ds(start, tile), :], fac_ref[span, :]
                )
            else:
                value = None
            for q in range(start // stretch, last + 1):
                for p in range(low, low + pair):
                    place = pl.ds(q * stretch * n_row + p, stretch, stride=n_row)
                    if q * n_row + n_row - 1 < p * n_col:
                        trail_ref[place, :] = jnp.zeros((stretch, stretch), jnp.float32)
                    else:
                        top = q * stretch - start
                        side = (p - low) * stretch
                        part = value[top : top + stretch, side : side + stretch]
                        gap = (p * n_col + col_at - q * n_row - row_at) * stretch
                        trail_ref[place, :] = jnp.where(ahead >= gap, part, 0.0)


def shards(teacher, panel_ids, rest_ids, inverse):
    n_row = lax.axis_size("row")
    n_col = lax.axis_size("col")
    stretch = rest_ids.shape[2]
    width = inverse.shape[0]
    panel, row_ids, col_ids = exchange(rest_ids, panel_ids, n_row, n_col)
    ids = jnp.concatenate([panel.reshape(-1), row_ids.reshape(-1), col_ids.reshape(-1)])
    emb = teacher.at[ids].get(mode="promise_in_bounds")
    total = emb.shape[0] - width
    vmem = pl.BlockSpec(memory_space=pltpu.VMEM)
    trailing, own_factor = pl.pallas_call(
        functools.partial(gram_kernel, n_row, n_col, stretch),
        out_shape=(
            jax.ShapeDtypeStruct((n_col * stretch * n_row, stretch), jnp.float32),
            jax.ShapeDtypeStruct((stretch, width), jnp.bfloat16),
        ),
        in_specs=[vmem, pl.BlockSpec(memory_space=pltpu.HBM)],
        out_specs=(vmem, vmem),
        scratch_shapes=[
            pltpu.VMEM((width, width), jnp.bfloat16),
            pltpu.VMEM((512, width), jnp.bfloat16),
            pltpu.VMEM((total, width), jnp.bfloat16),
            pltpu.VMEM((8, width), jnp.float32),
            pltpu.SemaphoreType.DMA((width // 256,)),
        ],
        compiler_params=pltpu.CompilerParams(vmem_limit_bytes=56 * 1024 * 1024),
        name="gram",
    )(emb, inverse)
    return (
        trailing.reshape(n_col, 1, stretch, n_row, 1, stretch),
        own_factor.reshape(1, 1, stretch, width),
    )


def solution(mesh):
    return jax.shard_map(
        shards,
        mesh=mesh,
        in_specs=(P(), P("col"), P("row", "col", None), P()),
        out_specs=(P(None, "row", None, None, "col", None), P("row", "col", None, None)),
        check_vma=False,
    )
```

```python
import functools

import jax
import jax.numpy as jnp
from jax import lax
from jax.experimental import pallas as pl
from jax.experimental.pallas import tpu as pltpu
from jax.sharding import PartitionSpec as P

MESH = pl.DeviceIdType.MESH


def exchange_kernel(
    n_row, n_col, rest_ref, panel_ref, table_hbm, emb_ref,
    panel_out, row_out, col_out, panel_ids, row_ids, col_ids, landed, table, picked,
    send_sem, row_sem, col_sem, panel_sem, table_sem, ids_sem,
):
    pieces = table_sem.shape[0]
    piece = table_hbm.shape[0] // pieces

    def load(at):
        rows = pl.ds(at * piece, piece)
        return pltpu.make_async_copy(table_hbm.at[rows], landed.at[rows], table_sem.at[at])

    for at in range(pieces):
        load(at).start()
    row_at = lax.axis_index("row")
    col_at = lax.axis_index("col")
    me = row_at * n_col + col_at
    barrier = pltpu.get_barrier_semaphore()
    count = n_row * n_col

    def greet(step, carry):
        other = lax.rem(me + step, count)
        pl.semaphore_signal(
            barrier, inc=1, device_id=(other // n_col, lax.rem(other, n_col)), device_id_type=MESH
        )
        return carry

    lax.fori_loop(1, count, greet, 0)
    panel_out[col_at] = panel_ref[0]
    col_out[row_at] = rest_ref[0]
    row_role = lax.rem(me, n_row)
    place = me // n_row

    @pl.when(row_role == row_at)
    def _():
        row_out[place] = rest_ref[0]

    pl.semaphore_wait(barrier, count - 1)

    def panel_copy(slot, target):
        return pltpu.make_async_remote_copy(
            src_ref=panel_ref.at[0], dst_ref=panel_out.at[slot],
            send_sem=send_sem.at[target], recv_sem=panel_sem.at[slot],
            device_id=(row_at, target), device_id_type=MESH,
        )

    def row_copy(slot, target):
        return pltpu.make_async_remote_copy(
            src_ref=rest_ref.at[0], dst_ref=row_out.at[slot],
            send_sem=send_sem.at[n_col + target], recv_sem=row_sem.at[slot],
            device_id=(row_role, target), device_id_type=MESH,
        )

    def col_copy(slot, target):
        return pltpu.make_async_remote_copy(
            src_ref=rest_ref.at[0], dst_ref=col_out.at[slot],
            send_sem=send_sem.at[2 * n_col + target], recv_sem=col_sem.at[slot],
            device_id=(target, col_at), device_id_type=MESH,
        )

    def each(length, skip, act):
        for at in range(length):
            pl.when(jnp.logical_not(skip(at)))(functools.partial(act, at))

    to_self = lambda at: jnp.logical_and(row_role == row_at, at == col_at)
    from_self = lambda at: at * n_row + row_at == me
    each(n_col, lambda at: at == col_at, lambda at: panel_copy(col_at, at).start())
    each(n_col, to_self, lambda at: row_copy(place, at).start())
    each(n_row, lambda at: at == row_at, lambda at: col_copy(row_at, at).start())
    for at in range(pieces):
        load(at).wait()

        def widen(step, carry, at=at):
            rows = pl.ds(pl.multiple_of(at * piece + step * 64, 64), 64)
            table[rows, :] = landed[rows, :].astype(jnp.float32)
            return carry

        lax.fori_loop(0, piece // 64, widen, 0)
    each(n_col, lambda at: at == col_at, lambda at: panel_copy(at, at).wait_recv())
    each(n_col, from_self, lambda at: row_copy(at, at).wait_recv())
    each(n_row, lambda at: at == row_at, lambda at: col_copy(at, at).wait_recv())
    each(n_col, lambda at: at == col_at, lambda at: panel_copy(col_at, at).wait_send())
    each(n_col, to_self, lambda at: row_copy(place, at).wait_send())
    each(n_row, lambda at: at == row_at, lambda at: col_copy(row_at, at).wait_send())
    groups = ((panel_out, panel_ids), (row_out, row_ids), (col_out, col_ids))
    moves = [pltpu.make_async_copy(src, dst, ids_sem.at[at]) for at, (src, dst) in enumerate(groups)]
    for move in moves:
        move.start()
    for move in moves:
        move.wait()
    unroll = 16
    first = 0
    for _, ids in groups:
        count, _, span = ids.shape

        def pick(step, carry, ids=ids, span=span, first=first):
            at = step * unroll
            block, inner = at // span, lax.rem(at, span)
            for lane in range(unroll):
                row = ids[block, 0, inner + lane]
                picked[pl.ds(pl.multiple_of(first + at, unroll) + lane, 1), :] = table[pl.ds(row, 1), :]
            return carry

        lax.fori_loop(0, count * span // unroll, pick, 0)
        first += count * span

    def narrow(step, carry):
        rows = pl.ds(pl.multiple_of(step * 64, 64), 64)
        emb_ref[rows, :] = picked[rows, :].astype(jnp.bfloat16)
        return carry

    lax.fori_loop(0, first // 64, narrow, 0)


def exchange(rest_ids, panel_ids, teacher, n_row, n_col):
    stretch = rest_ids.shape[2]
    width = panel_ids.shape[0]
    total = n_col * width + (n_col + n_row) * stretch
    shapes = ((n_col, 1, width), (n_col, 1, stretch), (n_row, 1, stretch))
    vmem = pl.BlockSpec(memory_space=pltpu.VMEM)
    return pl.pallas_call(
        functools.partial(exchange_kernel, n_row, n_col),
        out_shape=jax.ShapeDtypeStruct((total, teacher.shape[1]), teacher.dtype),
        in_specs=[vmem, vmem, pl.BlockSpec(memory_space=pltpu.HBM)],
        out_specs=vmem,
        scratch_shapes=[pltpu.VMEM(shape, jnp.int32) for shape in shapes]
        + [pltpu.SMEM(shape, jnp.int32) for shape in shapes]
        + [
            pltpu.VMEM(teacher.shape, teacher.dtype),
            pltpu.VMEM(teacher.shape, jnp.float32),
            pltpu.VMEM((total, teacher.shape[1]), jnp.float32),
            pltpu.SemaphoreType.DMA((2 * n_col + n_row,)),
            pltpu.SemaphoreType.DMA((n_col,)),
            pltpu.SemaphoreType.DMA((n_row,)),
            pltpu.SemaphoreType.DMA((n_col,)),
            pltpu.SemaphoreType.DMA((8,)),
            pltpu.SemaphoreType.DMA((3,)),
        ],
        compiler_params=pltpu.CompilerParams(
            collective_id=0, has_side_effects=True, vmem_limit_bytes=52 * 1024 * 1024
        ),
        name="exchange",
    )(rest_ids, panel_ids.reshape(1, 1, width), teacher)


def nt_dot(left, right):
    return lax.dot_general(left, right, (((1,), (1,)), ((), ())), preferred_element_type=jnp.float32)


def gram_kernel(n_row, n_col, stretch, emb_ref, inv_hbm, trail_ref, own_ref, inv_ref, cross_ref, fac_ref, norm_ref, inv_sem):
    width = inv_hbm.shape[0]
    block = 256
    blocks = width // block
    total = emb_ref.shape[0] - width
    n_rows = n_col * stretch
    unit = 2.0 / emb_ref.shape[1] * 1.4426950408889634
    row_at = lax.axis_index("row")
    col_at = lax.axis_index("col")

    def load(at):
        rows, cols = pl.ds(at * block, block), pl.ds(0, (at + 1) * block)
        return pltpu.make_async_copy(inv_hbm.at[rows, cols], inv_ref.at[rows, cols], inv_sem.at[at])

    for at in range(blocks):
        load(at).start()

    def across(value):
        square = jnp.square(value.astype(jnp.float32))
        high = square.astype(jnp.bfloat16)
        low = (square - high.astype(jnp.float32)).astype(jnp.bfloat16)
        ones = jnp.ones((8, value.shape[1]), jnp.bfloat16)
        return (nt_dot(ones, high) + nt_dot(ones, low)) * unit

    def down(value):
        return jnp.sum(jnp.square(value.astype(jnp.float32)), axis=-1, keepdims=True) * unit

    for at in range(blocks):
        norm_ref[:, at * block : (at + 1) * block] = across(emb_ref[at * block : (at + 1) * block, :])

    def gram(left, left_norm, right, right_norm):
        return jnp.exp2(nt_dot(left, right) * (2.0 * unit) - (left_norm + right_norm))

    tile = 512

    def factor_tile(start, first):
        rows = pl.ds(start, tile)
        left = emb_ref[pl.ds(width + start, tile), :]
        left_norm = down(left)
        for at in range(blocks):
            cols = slice(at * block, (at + 1) * block)
            cross_ref[:, cols] = gram(left, left_norm, emb_ref[cols, :], norm_ref[0:1, cols]).astype(jnp.bfloat16)
            if first:
                load(at).wait()
            fac_ref[rows, cols] = nt_dot(
                cross_ref[:, : (at + 1) * block], inv_ref[cols, : (at + 1) * block]
            ).astype(jnp.bfloat16)

    factor_tile(n_rows, True)
    for start in range(n_rows + tile, total, tile):
        factor_tile(start, False)
    own_ref[...] = fac_ref[pl.ds(pl.multiple_of(n_rows + row_at * stretch, stretch), stretch), :]

    ahead = lax.broadcasted_iota(jnp.int32, (stretch, stretch), 0) - lax.broadcasted_iota(
        jnp.int32, (stretch, stretch), 1
    )
    pair = 2 if n_row % 2 == 0 else 1
    for start in range(0, n_rows, tile):
        factor_tile(start, False)
        left = emb_ref[pl.ds(width + start, tile), :]
        left_norm = down(left)
        last = (start + tile) // stretch - 1
        for low in range(0, n_row, pair):
            if last * n_row + n_row - 1 >= low * n_col:
                first_col = n_rows + low * stretch
                span = pl.ds(first_col, pair * stretch)
                right = emb_ref[pl.ds(width + first_col, pair * stretch), :]
                value = gram(left, left_norm, right, across(right)[0:1]) - nt_dot(
                    fac_ref[pl.ds(start, tile), :], fac_ref[span, :]
                )
            else:
                value = None
            for q in range(start // stretch, last + 1):
                for p in range(low, low + pair):
                    place = pl.ds(q * stretch * n_row + p, stretch, stride=n_row)
                    if q * n_row + n_row - 1 < p * n_col:
                        trail_ref[place, :] = jnp.zeros((stretch, stretch), jnp.float32)
                    else:
                        top = q * stretch - start
                        side = (p - low) * stretch
                        part = value[top : top + stretch, side : side + stretch]
                        gap = (p * n_col + col_at - q * n_row - row_at) * stretch
                        trail_ref[place, :] = jnp.where(ahead >= gap, part, 0.0)


def shards(teacher, panel_ids, rest_ids, inverse):
    n_row = lax.axis_size("row")
    n_col = lax.axis_size("col")
    stretch = rest_ids.shape[2]
    width = inverse.shape[0]
    emb = exchange(rest_ids, panel_ids, teacher, n_row, n_col)
    total = emb.shape[0] - width
    vmem = pl.BlockSpec(memory_space=pltpu.VMEM)
    trailing, own_factor = pl.pallas_call(
        functools.partial(gram_kernel, n_row, n_col, stretch),
        out_shape=(
            jax.ShapeDtypeStruct((n_col * stretch * n_row, stretch), jnp.float32),
            jax.ShapeDtypeStruct((stretch, width), jnp.bfloat16),
        ),
        in_specs=[vmem, pl.BlockSpec(memory_space=pltpu.HBM)],
        out_specs=(vmem, vmem),
        scratch_shapes=[
            pltpu.VMEM((width, width), jnp.bfloat16),
            pltpu.VMEM((512, width), jnp.bfloat16),
            pltpu.VMEM((total, width), jnp.bfloat16),
            pltpu.VMEM((8, width), jnp.float32),
            pltpu.SemaphoreType.DMA((width // 256,)),
        ],
        compiler_params=pltpu.CompilerParams(vmem_limit_bytes=50 * 1024 * 1024),
        name="gram",
    )(emb, inverse)
    return (
        trailing.reshape(n_col, 1, stretch, n_row, 1, stretch),
        own_factor.reshape(1, 1, stretch, width),
    )


def solution(mesh):
    return jax.shard_map(
        shards,
        mesh=mesh,
        in_specs=(P(), P("col"), P("row", "col", None), P()),
        out_specs=(P(None, "row", None, None, "col", None), P("row", "col", None, None)),
        check_vma=False,
    )
```

```python
import functools

import jax
import jax.numpy as jnp
from jax import lax
from jax.experimental import pallas as pl
from jax.experimental.pallas import tpu as pltpu
from jax.sharding import PartitionSpec as P

MESH = pl.DeviceIdType.MESH


def exchange_kernel(
    n_row, n_col, rest_ref, panel_ref, table_hbm, emb_ref,
    panel_out, row_out, col_out, panel_ids, row_ids, col_ids, landed, table, picked,
    send_sem, row_sem, col_sem, panel_sem, table_sem, ids_sem,
):
    pieces = table_sem.shape[0]
    lanes = table.shape[1]
    halves = table_hbm.shape[1] // lanes
    piece = table_hbm.shape[0] // pieces

    def load(at):
        rows = pl.ds(at * piece, piece)
        return pltpu.make_async_copy(table_hbm.at[rows], landed.at[rows], table_sem.at[at])

    for at in range(pieces):
        load(at).start()
    row_at = lax.axis_index("row")
    col_at = lax.axis_index("col")
    me = row_at * n_col + col_at
    barrier = pltpu.get_barrier_semaphore()
    count = n_row * n_col

    def greet(step, carry):
        other = lax.rem(me + step, count)
        pl.semaphore_signal(
            barrier, inc=1, device_id=(other // n_col, lax.rem(other, n_col)), device_id_type=MESH
        )
        return carry

    lax.fori_loop(1, count, greet, 0)
    panel_out[col_at] = panel_ref[0]
    col_out[row_at] = rest_ref[0]
    row_role = lax.rem(me, n_row)
    place = me // n_row

    @pl.when(row_role == row_at)
    def _():
        row_out[place] = rest_ref[0]

    pl.semaphore_wait(barrier, count - 1)

    def panel_copy(slot, target):
        return pltpu.make_async_remote_copy(
            src_ref=panel_ref.at[0], dst_ref=panel_out.at[slot],
            send_sem=send_sem.at[target], recv_sem=panel_sem.at[slot],
            device_id=(row_at, target), device_id_type=MESH,
        )

    def row_copy(slot, target):
        return pltpu.make_async_remote_copy(
            src_ref=rest_ref.at[0], dst_ref=row_out.at[slot],
            send_sem=send_sem.at[n_col + target], recv_sem=row_sem.at[slot],
            device_id=(row_role, target), device_id_type=MESH,
        )

    def col_copy(slot, target):
        return pltpu.make_async_remote_copy(
            src_ref=rest_ref.at[0], dst_ref=col_out.at[slot],
            send_sem=send_sem.at[2 * n_col + target], recv_sem=col_sem.at[slot],
            device_id=(target, col_at), device_id_type=MESH,
        )

    def each(length, skip, act):
        for at in range(length):
            pl.when(jnp.logical_not(skip(at)))(functools.partial(act, at))

    to_self = lambda at: jnp.logical_and(row_role == row_at, at == col_at)
    from_self = lambda at: at * n_row + row_at == me
    each(n_col, lambda at: at == col_at, lambda at: panel_copy(col_at, at).start())
    each(n_col, to_self, lambda at: row_copy(place, at).start())
    each(n_row, lambda at: at == row_at, lambda at: col_copy(row_at, at).start())
    for at in range(pieces):
        load(at).wait()

        def widen(step, carry, at=at):
            rows = pl.ds(pl.multiple_of(at * piece + step * 64, 64), 64)
            wide = landed[rows, :].astype(jnp.float32)
            for half in range(halves):
                place = pl.ds((at * piece + step * 64) * halves + half, 64, stride=halves)
                table[place, :] = wide[:, half * lanes : (half + 1) * lanes]
            return carry

        lax.fori_loop(0, piece // 64, widen, 0)
    each(n_col, lambda at: at == col_at, lambda at: panel_copy(at, at).wait_recv())
    each(n_col, from_self, lambda at: row_copy(at, at).wait_recv())
    each(n_row, lambda at: at == row_at, lambda at: col_copy(at, at).wait_recv())
    each(n_col, lambda at: at == col_at, lambda at: panel_copy(col_at, at).wait_send())
    each(n_col, to_self, lambda at: row_copy(place, at).wait_send())
    each(n_row, lambda at: at == row_at, lambda at: col_copy(row_at, at).wait_send())
    groups = ((panel_out, panel_ids), (row_out, row_ids), (col_out, col_ids))
    moves = [pltpu.make_async_copy(src, dst, ids_sem.at[at]) for at, (src, dst) in enumerate(groups)]
    for move in moves:
        move.start()
    for move in moves:
        move.wait()
    first = 0
    for _, ids in groups:
        count, _, span = ids.shape

        def pick(block, carry, ids=ids, span=span, first=first):
            start = pl.multiple_of((first + block * span) * halves, span * halves)
            home = picked.at[pl.ds(start, span * halves)]
            for lane in range(span):
                row = ids[block, 0, lane] * halves
                home[lane * halves : (lane + 1) * halves, :] = table[pl.ds(row, halves), :]
            return carry

        lax.fori_loop(0, count, pick, 0)
        first += count * span

    def narrow(step, carry):
        rows = pl.ds(pl.multiple_of(step * 64, 64), 64)
        for half in range(halves):
            value = picked[pl.ds(step * 64 * halves + half, 64, stride=halves), :]
            emb_ref[rows, half * lanes : (half + 1) * lanes] = value.astype(jnp.bfloat16)
        return carry

    lax.fori_loop(0, first // 64, narrow, 0)


def exchange(rest_ids, panel_ids, teacher, n_row, n_col):
    stretch = rest_ids.shape[2]
    width = panel_ids.shape[0]
    total = n_col * width + (n_col + n_row) * stretch
    shapes = ((n_col, 1, width), (n_col, 1, stretch), (n_row, 1, stretch))
    vmem = pl.BlockSpec(memory_space=pltpu.VMEM)
    return pl.pallas_call(
        functools.partial(exchange_kernel, n_row, n_col),
        out_shape=jax.ShapeDtypeStruct((total, teacher.shape[1]), teacher.dtype),
        in_specs=[vmem, vmem, pl.BlockSpec(memory_space=pltpu.HBM)],
        out_specs=vmem,
        scratch_shapes=[pltpu.VMEM(shape, jnp.int32) for shape in shapes]
        + [pltpu.SMEM(shape, jnp.int32) for shape in shapes]
        + [
            pltpu.VMEM(teacher.shape, teacher.dtype),
            pltpu.VMEM((teacher.size // 128, 128), jnp.float32),
            pltpu.VMEM((total * teacher.shape[1] // 128, 128), jnp.float32),
            pltpu.SemaphoreType.DMA((2 * n_col + n_row,)),
            pltpu.SemaphoreType.DMA((n_col,)),
            pltpu.SemaphoreType.DMA((n_row,)),
            pltpu.SemaphoreType.DMA((n_col,)),
            pltpu.SemaphoreType.DMA((8,)),
            pltpu.SemaphoreType.DMA((3,)),
        ],
        compiler_params=pltpu.CompilerParams(
            collective_id=0, has_side_effects=True, vmem_limit_bytes=52 * 1024 * 1024
        ),
        name="exchange",
    )(rest_ids, panel_ids.reshape(1, 1, width), teacher)


def nt_dot(left, right):
    return lax.dot_general(left, right, (((1,), (1,)), ((), ())), preferred_element_type=jnp.float32)


def gram_kernel(n_row, n_col, stretch, emb_ref, inv_hbm, trail_ref, own_ref, inv_ref, cross_ref, fac_ref, norm_ref, inv_sem):
    width = inv_hbm.shape[0]
    block = 256
    blocks = width // block
    total = emb_ref.shape[0] - width
    n_rows = n_col * stretch
    unit = 2.0 / emb_ref.shape[1] * 1.4426950408889634
    row_at = lax.axis_index("row")
    col_at = lax.axis_index("col")

    def load(at):
        rows, cols = pl.ds(at * block, block), pl.ds(0, (at + 1) * block)
        return pltpu.make_async_copy(inv_hbm.at[rows, cols], inv_ref.at[rows, cols], inv_sem.at[at])

    for at in range(blocks):
        load(at).start()

    def across(value):
        square = jnp.square(value.astype(jnp.float32))
        high = square.astype(jnp.bfloat16)
        low = (square - high.astype(jnp.float32)).astype(jnp.bfloat16)
        ones = jnp.ones((8, value.shape[1]), jnp.bfloat16)
        return (nt_dot(ones, high) + nt_dot(ones, low)) * unit

    def down(value):
        return jnp.sum(jnp.square(value.astype(jnp.float32)), axis=-1, keepdims=True) * unit

    for at in range(blocks):
        norm_ref[:, at * block : (at + 1) * block] = across(emb_ref[at * block : (at + 1) * block, :])

    def gram(left, left_norm, right, right_norm):
        return jnp.exp2(nt_dot(left, right) * (2.0 * unit) - (left_norm + right_norm))

    tile = 512

    def factor_tile(start, first):
        rows = pl.ds(start, tile)
        left = emb_ref[pl.ds(width + start, tile), :]
        left_norm = down(left)
        for at in range(blocks):
            cols = slice(at * block, (at + 1) * block)
            cross_ref[:, cols] = gram(left, left_norm, emb_ref[cols, :], norm_ref[0:1, cols]).astype(jnp.bfloat16)
            if first:
                load(at).wait()
            fac_ref[rows, cols] = nt_dot(
                cross_ref[:, : (at + 1) * block], inv_ref[cols, : (at + 1) * block]
            ).astype(jnp.bfloat16)

    factor_tile(n_rows, True)
    for start in range(n_rows + tile, total, tile):
        factor_tile(start, False)
    own_ref[...] = fac_ref[pl.ds(pl.multiple_of(n_rows + row_at * stretch, stretch), stretch), :]

    ahead = lax.broadcasted_iota(jnp.int32, (stretch, stretch), 0) - lax.broadcasted_iota(
        jnp.int32, (stretch, stretch), 1
    )
    pair = 2 if n_row % 2 == 0 else 1
    for start in range(0, n_rows, tile):
        factor_tile(start, False)
        left = emb_ref[pl.ds(width + start, tile), :]
        left_norm = down(left)
        last = (start + tile) // stretch - 1
        for low in range(0, n_row, pair):
            if last * n_row + n_row - 1 >= low * n_col:
                first_col = n_rows + low * stretch
                span = pl.ds(first_col, pair * stretch)
                right = emb_ref[pl.ds(width + first_col, pair * stretch), :]
                value = gram(left, left_norm, right, across(right)[0:1]) - nt_dot(
                    fac_ref[pl.ds(start, tile), :], fac_ref[span, :]
                )
            else:
                value = None
            for q in range(start // stretch, last + 1):
                for p in range(low, low + pair):
                    place = pl.ds(q * stretch * n_row + p, stretch, stride=n_row)
                    if q * n_row + n_row - 1 < p * n_col:
                        trail_ref[place, :] = jnp.zeros((stretch, stretch), jnp.float32)
                    else:
                        top = q * stretch - start
                        side = (p - low) * stretch
                        part = value[top : top + stretch, side : side + stretch]
                        gap = (p * n_col + col_at - q * n_row - row_at) * stretch
                        trail_ref[place, :] = jnp.where(ahead >= gap, part, 0.0)


def shards(teacher, panel_ids, rest_ids, inverse):
    n_row = lax.axis_size("row")
    n_col = lax.axis_size("col")
    stretch = rest_ids.shape[2]
    width = inverse.shape[0]
    emb = exchange(rest_ids, panel_ids, teacher, n_row, n_col)
    total = emb.shape[0] - width
    vmem = pl.BlockSpec(memory_space=pltpu.VMEM)
    trailing, own_factor = pl.pallas_call(
        functools.partial(gram_kernel, n_row, n_col, stretch),
        out_shape=(
            jax.ShapeDtypeStruct((n_col * stretch * n_row, stretch), jnp.float32),
            jax.ShapeDtypeStruct((stretch, width), jnp.bfloat16),
        ),
        in_specs=[vmem, pl.BlockSpec(memory_space=pltpu.HBM)],
        out_specs=(vmem, vmem),
        scratch_shapes=[
            pltpu.VMEM((width, width), jnp.bfloat16),
            pltpu.VMEM((512, width), jnp.bfloat16),
            pltpu.VMEM((total, width), jnp.bfloat16),
            pltpu.VMEM((8, width), jnp.float32),
            pltpu.SemaphoreType.DMA((width // 256,)),
        ],
        compiler_params=pltpu.CompilerParams(vmem_limit_bytes=50 * 1024 * 1024),
        name="gram",
    )(emb, inverse)
    return (
        trailing.reshape(n_col, 1, stretch, n_row, 1, stretch),
        own_factor.reshape(1, 1, stretch, width),
    )


def solution(mesh):
    return jax.shard_map(
        shards,
        mesh=mesh,
        in_specs=(P(), P("col"), P("row", "col", None), P()),
        out_specs=(P(None, "row", None, None, "col", None), P("row", "col", None, None)),
        check_vma=False,
    )
```
